32 devices in a mesh: gx: 8 (over z, core), gy: 4 (over y, x).
Axes of the slice: x: 2, y: 2, z: 4, core: 2. Of those that a mesh axis runs over, the one named last changes fastest.
Arguments:
- load: float32 [8, 4, 320, 768], P('gx', 'gy'), may hold values from -6 to 6
- stiffness: bfloat16 [8, 4, 768, 768], P('gx', 'gy'), may hold values from -0.5 to 3, as said below
- local_inverse: bfloat16 [8, 4, 768, 768], P('gx', 'gy'), may hold values from -0.5 to 3, as said below
- phi: float32 [8, 4, 8, 768], P('gx', 'gy'), may hold values from -2.5 to 2.5
- level2_inverse: float32 [8, 32, 32], P('gx'), may hold values from -0.5 to 3, as said below
- level3_inverse: bfloat16 [128, 128], replicated, may hold values from -0.5 to 3, as said below
- aggregate: int32 [8, 4], P('gx', 'gy'), may hold values from 0 to 1
Outputs:
- solution: float32 [8, 4, 320, 768], P('gx', 'gy')
The draws below stay inside these ranges and needn't reach their ends.
Inputs may be any that keep to these rules, and one draw needn't show every extreme that they name: `stiffness`: every block is symmetric positive definite. `local_inverse`: every block is symmetric positive definite. `level2_inverse`: every block is symmetric positive definite. `level3_inverse`: symmetric positive definite.
All inputs are finite; a program needn't handle non-finite values.
Results may differ from the reference program's by a relative error of at most 0.0091.
Values may be sent and summed in bfloat16 or wider, within the bound.
A program may use at most 64 MiB of HBM per device.

```python
import math
import jax
import jax.numpy as jnp
from jax import lax

NRHS = 320
P_SIZE = 8
NAGG = 2
ITERS = 2
M = 768
L2 = 32
L3 = 128
N_GX = 8
N_GY = 4


def spd_blocks(key, lead, order, salt):
    base = jax.random.fold_in(key, salt)
    first, second = jax.random.split(base)
    noise = jax.random.normal(first, lead + (order, order), jnp.float32)
    sym = (noise + jnp.swapaxes(noise, -1, -2)) * (0.35 / (2.0 * math.sqrt(order)))
    diag = jax.random.uniform(second, lead + (order,), jnp.float32, 1.0, 2.0)
    return sym + diag[..., None] * jnp.eye(order, dtype=jnp.float32)


def draw_stiffness(key, part):
    return spd_blocks(key, (N_GX, N_GY), M, 11).astype(jnp.bfloat16)


def draw_local_inverse(key, part):
    return spd_blocks(key, (N_GX, N_GY), M, 23).astype(jnp.bfloat16)


def draw_level2_inverse(key, part):
    return spd_blocks(key, (N_GX,), L2, 37)


def draw_level3_inverse(key, part):
    return spd_blocks(key, (), L3, 41).astype(jnp.bfloat16)


def touch_ends(result, stream_key, low, top_value):
    dims = result.shape
    index_at = [jax.random.randint(jax.random.fold_in(stream_key, axis), (), 0, dims[axis]) for axis in range(len(dims))]
    result = result.at[tuple(index_at)].set(low)
    longest = dims.index(max(dims))
    index_at[longest] = (index_at[longest] + 1) % dims[longest]
    return result.at[tuple(index_at)].set(top_value)


def shard_levels(stream_key, shape, pieces, smallest, largest):
    loudness = 1.0
    for dim, blocks in pieces:
        steps = jax.random.uniform(jax.random.fold_in(jax.random.fold_in(stream_key, 6), dim), (blocks,), jnp.float32, smallest / len(pieces), largest / len(pieces))
        loudness = loudness * jnp.repeat(jnp.exp(steps), shape[dim] // blocks).reshape((-1,) + (1,) * (len(shape) - 1 - dim))
    return loudness


def bell_draw(rng, dims, spread, bound, cuts=(), kind=jnp.bfloat16):
    values = spread * jax.random.normal(rng, dims, jnp.float32)
    if cuts:
        values = values * shard_levels(rng, dims, cuts, -0.22, 0.18)
    return jnp.clip(values, -bound, bound).astype(kind)


def setup_inputs(seed: int = 0) -> dict:
    key_list = jax.random.split(jax.random.key(seed), 8)
    return {
        "load": bell_draw(key_list[0], (N_GX, N_GY, NRHS, M), 1.0, 6.0, ((0, 8), (1, 4)), jnp.float32),
        "stiffness": draw_stiffness(jax.random.fold_in(key_list[7], 71), 0),
        "local_inverse": draw_local_inverse(jax.random.fold_in(key_list[7], 71), 0),
        "phi": bell_draw(key_list[3], (N_GX, N_GY, P_SIZE, M), 0.16, 2.5, ((0, 8), (1, 4)), jnp.float32),
        "level2_inverse": draw_level2_inverse(jax.random.fold_in(key_list[7], 71), 0),
        "level3_inverse": draw_level3_inverse(jax.random.fold_in(key_list[7], 71), 0),
        "aggregate": touch_ends(jax.random.randint(key_list[6], (N_GX, N_GY), 0, NAGG), jax.random.fold_in(key_list[6], 1), 0, NAGG - 1).astype(jnp.int32),
    }


HIGH = lax.Precision.HIGHEST


def assemble(vec):
    width = M // 4
    edges = vec.reshape(N_GX, N_GY, NRHS, 4, width)
    west, east, south, north = edges[..., 0, :], edges[..., 1, :], edges[..., 2, :], edges[..., 3, :]
    new_west = west + jnp.concatenate([jnp.zeros_like(east[:1]), east[:-1]], axis=0)
    new_east = east + jnp.concatenate([west[1:], jnp.zeros_like(west[:1])], axis=0)
    new_south = south + jnp.concatenate([jnp.zeros_like(north[:, :1]), north[:, :-1]], axis=1)
    new_north = north + jnp.concatenate([south[:, 1:], jnp.zeros_like(south[:, :1])], axis=1)
    return jnp.stack([new_west, new_east, new_south, new_north], axis=3).reshape(N_GX, N_GY, NRHS, M)


def make_weights():
    width = M // 4
    col = jnp.broadcast_to(jnp.arange(N_GX, dtype=jnp.int32)[:, None], (N_GX, N_GY))
    row = jnp.broadcast_to(jnp.arange(N_GY, dtype=jnp.int32)[None, :], (N_GX, N_GY))
    edge_w = jnp.stack([jnp.where(col > 0, 0.5, 1.0), jnp.where(col < N_GX - 1, 0.5, 1.0),
                        jnp.where(row > 0, 0.5, 1.0), jnp.where(row < N_GY - 1, 0.5, 1.0)], axis=-1).astype(jnp.float32)
    return jnp.repeat(edge_w, width, axis=-1)[:, :, None, :]


def reference(load, stiffness, local_inverse, phi, level2_inverse, level3_inverse, aggregate):
    stiff32 = stiffness.astype(jnp.float32)
    inverse32 = local_inverse.astype(jnp.float32)
    top32 = level3_inverse.astype(jnp.float32)
    weights = make_weights()
    onehot = (aggregate[:, :, None] == jnp.arange(NAGG, dtype=jnp.int32)).astype(jnp.float32)

    def apply(vec):
        rounded = lax.optimization_barrier(vec.astype(jnp.bfloat16)).astype(jnp.float32)
        return assemble(jnp.einsum('abrm,abnm->abrn', rounded, stiff32, precision=HIGH))

    def precondition(resid):
        scaled = weights * resid
        rounded = lax.optimization_barrier(scaled.astype(jnp.bfloat16)).astype(jnp.float32)
        local = jnp.einsum('abrm,abnm->abrn', rounded, inverse32, precision=HIGH)
        primal = jnp.einsum('abrm,abpm->abrp', scaled, phi, precision=HIGH)
        grouped = primal.transpose(0, 2, 1, 3).reshape(N_GX, NRHS, L2)
        second = jnp.einsum('grk,glk->grl', grouped, level2_inverse, precision=HIGH)
        second = second.reshape(N_GX, NRHS, N_GY, P_SIZE).transpose(0, 2, 1, 3)
        summed = jnp.einsum('gbq,gbrp->grqp', onehot, primal, precision=HIGH)
        summed = summed.transpose(1, 0, 2, 3).reshape(NRHS, L3)
        summed = lax.optimization_barrier(summed.astype(jnp.bfloat16)).astype(jnp.float32)
        third = jnp.einsum('rl,kl->rk', summed, top32, precision=HIGH).reshape(NRHS, N_GX, NAGG, P_SIZE)
        third = jnp.einsum('gbq,rgqp->gbrp', onehot, third, precision=HIGH)
        full = local + jnp.einsum('abrp,abpm->abrm', second + third, phi, precision=HIGH)
        return assemble(weights * full)

    def inner(left, right):
        return jnp.sum(weights * left * right, axis=(0, 1, 3))

    rhs = assemble(load)
    solution = jnp.zeros_like(rhs)
    resid = rhs
    zvec = precondition(resid)
    svec = apply(zvec)
    pvec = zvec
    gamma = inner(resid, zvec)
    alpha = gamma / inner(pvec, svec)
    for step in range(ITERS):
        solution = solution + alpha[:, None] * pvec
        resid = resid - alpha[:, None] * svec
        if step < ITERS - 1:
            zvec = precondition(resid)
            wvec = apply(zvec)
            newer = inner(resid, zvec)
            beta = newer / gamma
            pvec = zvec + beta[:, None] * pvec
            svec = wvec + beta[:, None] * svec
            alpha = newer / inner(pvec, svec)
            gamma = newer
    return solution
```

```python
import functools

import jax
import jax.numpy as jnp
from jax import lax
from jax.experimental import pallas as pl
from jax.experimental.pallas import tpu as pltpu
from jax.sharding import PartitionSpec as P

NAGG = 2
CHUNKS = 1
HIGH = lax.Precision.HIGHEST
MESH = pl.DeviceIdType.MESH
F32 = jnp.float32
BF16 = jnp.bfloat16
NEAR = (("gx", -1), ("gx", 1), ("gy", -1), ("gy", 1))


def dot(left, right, dims, precision=None):
    return lax.dot_general(
        left, right, (dims, ((), ())), precision=precision, preferred_element_type=F32
    )


NT = ((1,), (1,))
NN = ((1,), (0,))
TN = ((0,), (0,))


def kernel(
    ngx, ngy, rows, total, prim,
    load_h, stiff_h, inv_h, phi_r, l2_r, l3_r, agg_r,
    out_h,
    load_v, stiff_v, inv_v, out_v, in_sem, out_sem,
    es, er, es_sem, er_sem,
    ps, pr, ps_sem, pr_sem, pbig,
    cg, cg_ss, cg_rs, eg, eg_ss, eg_rs, xs, xr, xs_sem, xr_sem,
    x2s, t3s,
    sa, sa_ss, sa_rs, sb, sb_ss, sb_rs,
    rr, ur, z0r, z1r, y0r, gp, cown, xown, tot,
):
    width = total // 4
    R = rows // CHUNKS
    block = NAGG * prim
    col = lax.axis_index("gx")
    row = lax.axis_index("gy")
    exists = (col > 0, col < ngx - 1, row > 0, row < ngy - 1)

    def near(e):
        axis, step = NEAR[e]
        return {axis: (col if axis == "gx" else row) + step}

    def load_copy(k):
        return pltpu.make_async_copy(
            load_h.at[0, 0, pl.ds(k * R, R)], load_v.at[pl.ds(k * R, R)], in_sem.at[2 + k]
        )

    for k in range(CHUNKS):
        load_copy(k).start()
    inv_copy = pltpu.make_async_copy(inv_h.at[0, 0], inv_v, in_sem.at[0])
    stiff_copy = pltpu.make_async_copy(stiff_h.at[0, 0], stiff_v, in_sem.at[1])
    inv_copy.start()
    stiff_copy.start()

    for e in range(4):
        @pl.when(jnp.logical_not(exists[e]))
        def _():
            er[:, :, e] = jnp.zeros((4, CHUNKS) + er.shape[3:], BF16)
            pr[e] = jnp.zeros(pr.shape[1:], F32)
            if e < 2:
                xr[:, :, e] = jnp.zeros((2, CHUNKS) + xr.shape[3:], F32)

    barrier = pltpu.get_barrier_semaphore()
    for d in range(1, ngx):
        pl.semaphore_signal(barrier, inc=1, device_id={"gx": lax.rem(col + d, ngx)}, device_id_type=MESH)
    for d in range(1, ngy):
        pl.semaphore_signal(barrier, inc=1, device_id={"gy": lax.rem(row + d, ngy)}, device_id_type=MESH)

    lane = lax.broadcasted_iota(jnp.int32, (1, total), 1)
    ew = [jnp.where(x, 0.5, 1.0).astype(F32) for x in exists]
    wrow = jnp.where(
        lane < 2 * width,
        jnp.where(lane < width, ew[0], ew[1]),
        jnp.where(lane < 3 * width, ew[2], ew[3]),
    )
    bases = (0, 128, 384, 512)
    lane128 = lax.broadcasted_iota(jnp.int32, (1, 128), 1)
    low = lane128 < 64
    low192 = lax.broadcasted_iota(jnp.int32, (1, 256), 1) < 192

    def aligned(x, e):
        part = x[:, bases[e]:bases[e] + 256]
        return pltpu.roll(part, 192, 1) if e % 2 else part

    def put_back(part, e):
        part = jnp.where(low192, part, 0.0)
        return pltpu.roll(part, 64, 1) if e % 2 else part

    def pack(x, e):
        a = aligned(x, e)
        first, second = a[:, :128], a[:, 128:]
        return first, jnp.where(low, second[: R // 2], pltpu.roll(second[R // 2:], 64, 1))

    def edge_copy(x, k, e):
        return pltpu.make_async_remote_copy(
            src_ref=es.at[x, k, e], dst_ref=er.at[x, k, e ^ 1],
            send_sem=es_sem.at[x, k, e], recv_sem=er_sem.at[x, k, e ^ 1],
            device_id=near(e), device_id_type=MESH,
        )

    def edge_wait(x, k, e):
        return pltpu.make_async_remote_copy(
            src_ref=es.at[x, k, e], dst_ref=er.at[x, k, e],
            send_sem=es_sem.at[x, k, e], recv_sem=er_sem.at[x, k, e],
            device_id=near(e), device_id_type=MESH,
        )

    def send_edges(x, k, value):
        for e in (2, 3, 0, 1):
            a, b = pack(value, e)
            es[x, k, e, :R] = a.astype(BF16)
            es[x, k, e, R:] = b.astype(BF16)

            @pl.when(exists[e])
            def _():
                edge_copy(x, k, e).start()

    def wait_edges(x, k):
        for e in (0, 1, 2, 3):
            @pl.when(exists[e])
            def _():
                edge_wait(x, k, e).wait_recv()

    def with_edges(x, k, value):
        added = []
        for e in range(4):
            a = er[x, k, e, :R].astype(F32)
            b = er[x, k, e, R:].astype(F32)
            b = jnp.concatenate([b, pltpu.roll(b, 64, 1)], axis=0)
            added.append(put_back(jnp.concatenate([a, b], axis=1), e))
        parts = []
        for s in range(2):
            first, second = added[2 * s], added[2 * s + 1]
            parts += [first[:, :128], first[:, 128:] + second[:, :128], second[:, 128:]]
        return value + jnp.concatenate(parts, axis=1)

    phi = phi_r[0, 0]
    phi_hi = phi.astype(BF16)
    phi_lo = (phi - phi_hi.astype(F32)).astype(BF16)
    phi2 = jnp.concatenate([phi_hi, phi_lo], axis=0)
    masks = [jnp.where(agg_r[0, 0] == q, 1.0, 0.0).astype(F32) for q in range(NAGG)]
    pown = jnp.concatenate([phi] + [phi * m for m in masks], axis=0) * wrow
    prow = pown.shape[0]
    pbig[...] = jnp.zeros_like(pbig)
    pbig[0:prow, :] = pown
    for e in range(4):
        ps[e] = aligned(pown, e)

    def base_copy(e, there):
        return pltpu.make_async_remote_copy(
            src_ref=ps.at[e], dst_ref=pr.at[there], send_sem=ps_sem.at[e], recv_sem=pr_sem.at[there],
            device_id=near(e), device_id_type=MESH,
        )

    pl.semaphore_wait(barrier, ngx - 1 + ngy - 1)

    def spread(buf, ssem, rsem, t, k, axis):
        me, n = (col, ngx) if axis == "gx" else (row, ngy)
        for d in range(1, n):
            pltpu.make_async_remote_copy(
                src_ref=buf.at[t, k, me], dst_ref=buf.at[t, k, me],
                send_sem=ssem.at[t, k, d], recv_sem=rsem.at[t, k, me],
                device_id={axis: lax.rem(me + d, n)}, device_id_type=MESH,
            ).start()

    def gathered(buf, ssem, rsem, t, k, axis):
        me, n = (col, ngx) if axis == "gx" else (row, ngy)
        for d in range(1, n):
            src = lax.rem(me + d, n)
            pltpu.make_async_remote_copy(
                src_ref=buf.at[t, k, src], dst_ref=buf.at[t, k, src],
                send_sem=ssem.at[t, k, d], recv_sem=rsem.at[t, k, src],
                device_id={axis: src}, device_id_type=MESH,
            ).wait_recv()

    def sent(buf, ssem, rsem, t, k, axis):
        me, n = (col, ngx) if axis == "gx" else (row, ngy)
        for d in range(1, n):
            pltpu.make_async_remote_copy(
                src_ref=buf.at[t, k, me], dst_ref=buf.at[t, k, me],
                send_sem=ssem.at[t, k, d], recv_sem=rsem.at[t, k, me],
                device_id={axis: lax.rem(me + d, n)}, device_id_type=MESH,
            ).wait_send()

    def x_copy(t, k, e, there):
        return pltpu.make_async_remote_copy(
            src_ref=xs.at[t, k], dst_ref=xr.at[t, k, there],
            send_sem=xs_sem.at[t, k, e], recv_sem=xr_sem.at[t, k, there],
            device_id=near(e), device_id_type=MESH,
        )

    def fold(v):
        acc = v[:, :128]
        for i in range(128, total, 128):
            acc = acc + v[:, i:i + 128]
        return acc

    def rows_of(parts):
        line = lax.broadcasted_iota(jnp.int32, (8, 128), 0)
        out = None
        for q, part in parts:
            one = dot(jnp.where(line == q, 1.0, 0.0).astype(F32), part, NT, HIGH)
            out = one if out is None else out + one
        return out

    def columns_of(values):
        n = len(values)
        line8 = lax.broadcasted_iota(jnp.int32, (8, R), 0)
        v = jnp.zeros((8, R), F32)
        for q, val in enumerate(values):
            v = jnp.where(line8 == q, val, v)
        line = lax.broadcasted_iota(jnp.int32, (8, 128 * n), 0)
        lanes = lax.broadcasted_iota(jnp.int32, (8, 128 * n), 1)
        pick = jnp.where((lanes >= line * 128) & (lanes < line * 128 + 128), 1.0, 0.0).astype(F32)
        c = dot(v, pick, TN, HIGH)
        return [c[:, 128 * q:128 * q + 128] for q in range(n)]

    def wide(c):
        return jnp.concatenate([c] * (total // 128), axis=1)

    def start(k):
        load_copy(k).wait()
        send_edges(0, k, load_v[pl.ds(k * R, R), :])

    def local_part(t, k, r):
        rs = wrow * r
        rsb = rs.astype(BF16)
        c = dot(phi2, rsb, NT)
        c = c[:prim] + c[prim:]
        cown[t, k] = c
        cg[t, k, row] = jnp.concatenate([c * m for m in masks], axis=0)
        spread(cg, cg_ss, cg_rs, t, k, "gy")
        if t == 0 and k == 0:
            inv_copy.wait()
        local = dot(rsb, inv_v[...], NN)
        u = wrow * local
        send_edges(1 + 2 * t, k, u)
        ur[t, k] = u
        gp[t, k] = fold(r * u)

    def first_local(k):
        wait_edges(0, k)
        r = with_edges(0, k, load_v[pl.ds(k * R, R), :])
        rr[k] = r
        local_part(0, k, r)

    def middle(t, k):
        gathered(cg, cg_ss, cg_rs, t, k, "gy")
        e = cg[t, k, 0]
        cs = [e[:prim] + e[prim:]]
        for j in range(1, ngy):
            o = cg[t, k, j]
            cs.append(o[:prim] + o[prim:])
            e = e + o
        eg[t, k, col] = e.astype(BF16)
        spread(eg, eg_ss, eg_rs, t, k, "gx")
        x2s[...] = dot(l2_r[0], jnp.concatenate(cs, axis=0), NN, HIGH)
        x2 = x2s[pl.ds(pl.multiple_of(row * prim, prim), prim), :]
        xs[t, k] = x2
        for e_ in range(2):
            @pl.when(exists[e_])
            def _():
                x_copy(t, k, e_, e_ ^ 1).start()
        before = x2s[pl.ds(pl.multiple_of(jnp.maximum(row - 1, 0) * prim, prim), prim), :]
        after = x2s[pl.ds(pl.multiple_of(jnp.minimum(row + 1, ngy - 1) * prim, prim), prim), :]
        xown[t, k, 0] = x2
        xown[t, k, 1] = before
        xown[t, k, 2] = after

    def direction(t, k):
        gathered(eg, eg_ss, eg_rs, t, k, "gx")
        e = jnp.concatenate([eg[t, k, i] for i in range(ngx)], axis=0)
        t3s[...] = dot(l3_r[...], e, NN)

        def t3(i):
            return t3s[pl.ds(pl.multiple_of(i * block, block), block), :]

        here, behind, ahead = t3(col), t3(jnp.maximum(col - 1, 0)), t3(jnp.minimum(col + 1, ngx - 1))
        for e_ in range(2):
            @pl.when(exists[e_])
            def _():
                x_copy(t, k, e_, e_).wait_recv()
        if t == 0 and k == 0:
            for e_ in range(4):
                @pl.when(exists[e_])
                def _():
                    base_copy(e_, e_).wait_recv()
                at = prow * (1 + e_)
                base = bases[e_]
                pbig[at:at + prow, base:base + 256] = put_back(pr[e_], e_)
        own = xown[t, k, 0]
        x = jnp.concatenate(
            [own, here, xr[t, k, 0], behind, xr[t, k, 1], ahead, xown[t, k, 1], here, xown[t, k, 2], here], axis=0
        )
        coarse = dot(x, pbig[...], TN, HIGH)
        full = own
        for q, m in enumerate(masks):
            full = full + m * here[q * prim:(q + 1) * prim]
        extra = jnp.sum(cown[t, k] * full, axis=0, keepdims=True)
        wait_edges(1 + 2 * t, k)
        z = with_edges(1 + 2 * t, k, ur[t, k] + coarse)
        return z, extra

    def message(t, k, parts, extra):
        m = rows_of(parts)
        line8 = lax.broadcasted_iota(jnp.int32, (8, R), 0)
        sa[t, k, row] = m + jnp.where(line8 == 0, extra, 0.0)
        spread(sa, sa_ss, sa_rs, t, k, "gy")

    def first_apply(k):
        z, extra = direction(0, k)
        if k == 0:
            stiff_copy.wait()
        y = dot(z.astype(BF16), stiff_v[...], NN)
        send_edges(2, k, y)
        message(0, k, [(0, gp[0, k]), (1, fold(z * y))], extra)
        z0r[k] = z
        y0r[k] = y

    def second_apply(k):
        z, extra = direction(1, k)
        y = dot(z.astype(BF16), stiff_v[...], NN)
        message(1, k, [(0, gp[1, k]), (1, fold(z * y)), (2, fold(z * y0r[k] + z0r[k] * y))], extra)
        z1r[k] = z

    def relay(t, k):
        gathered(sa, sa_ss, sa_rs, t, k, "gy")
        s = sa[t, k, 0]
        for j in range(1, ngy):
            s = s + sa[t, k, j]
        sb[t, k, col] = s
        spread(sb, sb_ss, sb_rs, t, k, "gx")

    def summed(t, k):
        gathered(sb, sb_ss, sb_rs, t, k, "gx")
        s = sb[t, k, 0]
        for j in range(1, ngx):
            s = s + sb[t, k, j]
        return s

    def second_local(k):
        s = summed(0, k)
        tot[k] = s
        alpha, = columns_of([s[0:1] / s[1:2]])
        wait_edges(2, k)
        r = rr[k] - wide(alpha) * with_edges(2, k, y0r[k])
        local_part(1, k, r)

    def out_copy(k):
        return pltpu.make_async_copy(out_v.at[pl.ds(k * R, R)], out_h.at[0, 0, pl.ds(k * R, R)], out_sem.at[k])

    def finish(k):
        s0, s1 = tot[k], summed(1, k)
        gamma, delta = s0[0:1], s0[1:2]
        new = s1[0:1]
        beta = new / gamma
        alpha1 = new / (s1[1:2] + beta * s1[2:3] + beta * beta * delta)
        first, second = columns_of([gamma / delta + alpha1 * beta, alpha1])
        out_v[pl.ds(k * R, R), :] = wide(first) * z0r[k] + wide(second) * z1r[k]
        out_copy(k).start()

    steps = [
        start, first_local, functools.partial(middle, 0), first_apply, functools.partial(relay, 0),
        second_local, functools.partial(middle, 1), second_apply, functools.partial(relay, 1), finish,
    ]
    for index, step in enumerate(steps):
        for k in range(CHUNKS):
            step(k)
        if index == 0:
            for e in range(4):
                @pl.when(exists[e])
                def _():
                    base_copy(e, e ^ 1).start()

    for k in range(CHUNKS):
        out_copy(k).wait()
        for e in range(4):
            @pl.when(exists[e])
            def _():
                for x in range(4):
                    edge_copy(x, k, e).wait_send()
                if k == 0:
                    base_copy(e, e ^ 1).wait_send()
                if e < 2:
                    for t in range(2):
                        x_copy(t, k, e, e ^ 1).wait_send()
        for t in range(2):
            sent(cg, cg_ss, cg_rs, t, k, "gy")
            sent(eg, eg_ss, eg_rs, t, k, "gx")
            sent(sa, sa_ss, sa_rs, t, k, "gy")
            sent(sb, sb_ss, sb_rs, t, k, "gx")


def body(load, stiffness, local_inverse, phi, level2_inverse, level3_inverse, aggregate):
    rows, total = load.shape[2:]
    prim = phi.shape[2]
    ngx, ngy = lax.axis_size("gx"), lax.axis_size("gy")
    R, C, block = rows // CHUNKS, CHUNKS, NAGG * prim
    prow = prim + block
    dma = pltpu.SemaphoreType.DMA
    vmem = pltpu.VMEM
    anyw = pl.BlockSpec(memory_space=pl.ANY)
    here = pl.BlockSpec(memory_space=pltpu.VMEM)
    scratch = [
        vmem((rows, total), F32), vmem((total, total), BF16), vmem((total, total), BF16), vmem((rows, total), F32),
        dma((2 + C,)), dma((C,)),
        vmem((4, C, 4, R + R // 2, 128), BF16), vmem((4, C, 4, R + R // 2, 128), BF16), dma((4, C, 4)), dma((4, C, 4)),
        vmem((4, prow, 256), F32), vmem((4, prow, 256), F32), dma((4,)), dma((4,)), vmem((5 * prow, total), F32),
        vmem((2, C, ngy, block, R), F32), dma((2, C, ngy)), dma((2, C, ngy)),
        vmem((2, C, ngx, block, R), BF16), dma((2, C, ngx)), dma((2, C, ngx)),
        vmem((2, C, prim, R), F32), vmem((2, C, 2, prim, R), F32), dma((2, C, 2)), dma((2, C, 2)),
        vmem((ngy * prim, R), F32), vmem((ngx * block, R), F32),
        vmem((2, C, ngy, 8, R), F32), dma((2, C, ngy)), dma((2, C, ngy)),
        vmem((2, C, ngx, 8, R), F32), dma((2, C, ngx)), dma((2, C, ngx)),
        vmem((C, R, total), F32), vmem((2, C, R, total), F32), vmem((C, R, total), F32), vmem((C, R, total), F32),
        vmem((C, R, total), F32), vmem((2, C, R, 128), F32), vmem((2, C, prim, R), F32), vmem((2, C, 3, prim, R), F32),
        vmem((C, 8, R), F32),
    ]
    return pl.pallas_call(
        functools.partial(kernel, ngx, ngy, rows, total, prim),
        out_shape=jax.ShapeDtypeStruct((1, 1, rows, total), F32),
        in_specs=[anyw, anyw, anyw, here, here, here, pl.BlockSpec(memory_space=pltpu.SMEM)],
        out_specs=anyw,
        scratch_shapes=scratch,
        compiler_params=pltpu.CompilerParams(
            collective_id=0, has_side_effects=True, vmem_limit_bytes=60 * 1024 * 1024
        ),
    )(load, stiffness, local_inverse, phi, level2_inverse, level3_inverse, aggregate)


def solution(mesh):
    return jax.shard_map(
        body,
        mesh=mesh,
        in_specs=(
            P("gx", "gy", None, None),
            P("gx", "gy", None, None),
            P("gx", "gy", None, None),
            P("gx", "gy", None, None),
            P("gx", None, None),
            P(),
            P("gx", "gy"),
        ),
        out_specs=P("gx", "gy", None, None),
        check_vma=False,
    )
```

```python
import functools

import jax
import jax.numpy as jnp
from jax import lax
from jax.experimental import pallas as pl
from jax.experimental.pallas import tpu as pltpu
from jax.sharding import PartitionSpec as P

NAGG = 2
CHUNKS = 1
HIGH = lax.Precision.HIGHEST
MESH = pl.DeviceIdType.MESH
F32 = jnp.float32
BF16 = jnp.bfloat16
NEAR = (("gx", -1), ("gx", 1), ("gy", -1), ("gy", 1))


def dot(left, right, dims, precision=None):
    return lax.dot_general(
        left, right, (dims, ((), ())), precision=precision, preferred_element_type=F32
    )


NT = ((1,), (1,))
NN = ((1,), (0,))
TN = ((0,), (0,))


def kernel(
    ngx, ngy, rows, total, prim,
    load_h, stiff_h, inv_h, phi_r, l2_r, l3_r, agg_r,
    out_h,
    load_v, stiff_v, inv_v, out_v, in_sem, out_sem,
    es, er, es_sem, er_sem,
    ps, pr, ps_sem, pr_sem, pbig, pbigb, pplain,
    ns, nr, ns_sem, nr_sem,
    cg, cg_ss, cg_rs, eg, eg_ss, eg_rs, xs, xr, xs_sem, xr_sem,
    x2s, t3s,
    sa, sa_ss, sa_rs, sb, sb_ss, sb_rs,
    rr, ur, z0r, z1r, y0r, gp, cown, xown, xall, xfull, tot,
):
    width = total // 4
    R = rows // CHUNKS
    block = NAGG * prim
    col = lax.axis_index("gx")
    row = lax.axis_index("gy")
    exists = (col > 0, col < ngx - 1, row > 0, row < ngy - 1)

    def near(e):
        axis, step = NEAR[e]
        return {axis: (col if axis == "gx" else row) + step}

    def load_copy(k):
        return pltpu.make_async_copy(
            load_h.at[0, 0, pl.ds(k * R, R)], load_v.at[pl.ds(k * R, R)], in_sem.at[2 + k]
        )

    for k in range(CHUNKS):
        load_copy(k).start()
    inv_copy = pltpu.make_async_copy(inv_h.at[0, 0], inv_v, in_sem.at[0])
    stiff_copy = pltpu.make_async_copy(stiff_h.at[0, 0], stiff_v, in_sem.at[1])
    inv_copy.start()
    stiff_copy.start()

    for e in range(4):
        @pl.when(jnp.logical_not(exists[e]))
        def _():
            er[:, :, e] = jnp.zeros((4, CHUNKS) + er.shape[3:], BF16)
            pr[e] = jnp.zeros(pr.shape[1:], F32)
            nr[:, e] = jnp.zeros((CHUNKS,) + nr.shape[2:], F32)
            if e < 2:
                xr[:, :, e] = jnp.zeros((2, CHUNKS) + xr.shape[3:], F32)

    barrier = pltpu.get_barrier_semaphore()
    for d in range(1, ngx):
        pl.semaphore_signal(barrier, inc=1, device_id={"gx": lax.rem(col + d, ngx)}, device_id_type=MESH)
    for d in range(1, ngy):
        pl.semaphore_signal(barrier, inc=1, device_id={"gy": lax.rem(row + d, ngy)}, device_id_type=MESH)

    lane = lax.broadcasted_iota(jnp.int32, (1, total), 1)
    ew = [jnp.where(x, 0.5, 1.0).astype(F32) for x in exists]
    wrow = jnp.where(
        lane < 2 * width,
        jnp.where(lane < width, ew[0], ew[1]),
        jnp.where(lane < 3 * width, ew[2], ew[3]),
    )
    bases = (0, 128, 384, 512)
    lane128 = lax.broadcasted_iota(jnp.int32, (1, 128), 1)
    low = lane128 < 64
    low192 = lax.broadcasted_iota(jnp.int32, (1, 256), 1) < 192

    def aligned(x, e):
        part = x[:, bases[e]:bases[e] + 256]
        return pltpu.roll(part, 192, 1) if e % 2 else part

    def put_back(part, e):
        part = jnp.where(low192, part, 0.0)
        return pltpu.roll(part, 64, 1) if e % 2 else part

    def pack(x, e):
        a = aligned(x, e)
        first, second = a[:, :128], a[:, 128:]
        return first, jnp.where(low, second[: R // 2], pltpu.roll(second[R // 2:], 64, 1))

    def edge_copy(x, k, e):
        return pltpu.make_async_remote_copy(
            src_ref=es.at[x, k, e], dst_ref=er.at[x, k, e ^ 1],
            send_sem=es_sem.at[x, k, e], recv_sem=er_sem.at[x, k, e ^ 1],
            device_id=near(e), device_id_type=MESH,
        )

    def edge_wait(x, k, e):
        return pltpu.make_async_remote_copy(
            src_ref=es.at[x, k, e], dst_ref=er.at[x, k, e],
            send_sem=es_sem.at[x, k, e], recv_sem=er_sem.at[x, k, e],
            device_id=near(e), device_id_type=MESH,
        )

    def send_edges(x, k, value):
        for e in (2, 3, 0, 1):
            a, b = pack(value, e)
            es[x, k, e, :R] = a.astype(BF16)
            es[x, k, e, R:] = b.astype(BF16)

            @pl.when(exists[e])
            def _():
                edge_copy(x, k, e).start()

    def wait_edges(x, k):
        for e in (0, 1, 2, 3):
            @pl.when(exists[e])
            def _():
                edge_wait(x, k, e).wait_recv()

    def with_edges(x, k, value):
        added = []
        for e in range(4):
            a = er[x, k, e, :R].astype(F32)
            b = er[x, k, e, R:].astype(F32)
            b = jnp.concatenate([b, pltpu.roll(b, 64, 1)], axis=0)
            added.append(put_back(jnp.concatenate([a, b], axis=1), e))
        parts = []
        for s in range(2):
            first, second = added[2 * s], added[2 * s + 1]
            parts += [first[:, :128], first[:, 128:] + second[:, :128], second[:, 128:]]
        return value + jnp.concatenate(parts, axis=1)

    phi = phi_r[0, 0]
    phi_hi = phi.astype(BF16)
    phi_lo = (phi - phi_hi.astype(F32)).astype(BF16)
    phi2 = jnp.concatenate([phi_hi, phi_lo], axis=0)
    masks = [jnp.where(agg_r[0, 0] == q, 1.0, 0.0).astype(F32) for q in range(NAGG)]
    pown = jnp.concatenate([phi] + [phi * m for m in masks], axis=0) * wrow
    prow = pown.shape[0]
    pbig[...] = jnp.zeros_like(pbig)
    pbig[0:prow, :] = pown
    for e in range(4):
        ps[e] = aligned(pown, e)

    def base_copy(e, there):
        return pltpu.make_async_remote_copy(
            src_ref=ps.at[e], dst_ref=pr.at[there], send_sem=ps_sem.at[e], recv_sem=pr_sem.at[there],
            device_id=near(e), device_id_type=MESH,
        )

    pl.semaphore_wait(barrier, ngx - 1 + ngy - 1)
    for e in range(4):
        @pl.when(exists[e])
        def _():
            base_copy(e, e ^ 1).start()

    def spread(buf, ssem, rsem, t, k, axis):
        me, n = (col, ngx) if axis == "gx" else (row, ngy)
        for d in range(1, n):
            pltpu.make_async_remote_copy(
                src_ref=buf.at[t, k, me], dst_ref=buf.at[t, k, me],
                send_sem=ssem.at[t, k, d], recv_sem=rsem.at[t, k, me],
                device_id={axis: lax.rem(me + d, n)}, device_id_type=MESH,
            ).start()

    def gathered(buf, ssem, rsem, t, k, axis):
        me, n = (col, ngx) if axis == "gx" else (row, ngy)
        for d in range(1, n):
            src = lax.rem(me + d, n)
            pltpu.make_async_remote_copy(
                src_ref=buf.at[t, k, src], dst_ref=buf.at[t, k, src],
                send_sem=ssem.at[t, k, d], recv_sem=rsem.at[t, k, src],
                device_id={axis: src}, device_id_type=MESH,
            ).wait_recv()

    def sent(buf, ssem, rsem, t, k, axis):
        me, n = (col, ngx) if axis == "gx" else (row, ngy)
        for d in range(1, n):
            pltpu.make_async_remote_copy(
                src_ref=buf.at[t, k, me], dst_ref=buf.at[t, k, me],
                send_sem=ssem.at[t, k, d], recv_sem=rsem.at[t, k, me],
                device_id={axis: lax.rem(me + d, n)}, device_id_type=MESH,
            ).wait_send()

    def x_copy(t, k, e, there):
        return pltpu.make_async_remote_copy(
            src_ref=xs.at[t, k], dst_ref=xr.at[t, k, there],
            send_sem=xs_sem.at[t, k, e], recv_sem=xr_sem.at[t, k, there],
            device_id=near(e), device_id_type=MESH,
        )

    def fold(v):
        acc = v[:, :128]
        for i in range(128, total, 128):
            acc = acc + v[:, i:i + 128]
        return acc

    def halves(v, axis):
        hi = v.astype(BF16)
        return jnp.concatenate([hi, (v - hi.astype(F32)).astype(BF16)], axis=axis)

    line8 = lax.broadcasted_iota(jnp.int32, (8, 128), 0)

    def tile_of(parts, extra):
        v = halves(jnp.concatenate(parts, axis=0), 1)
        line = lax.broadcasted_iota(jnp.int32, (8, 256), 0)
        out = jnp.zeros((8, 128), F32)
        for m in range(-(-v.shape[0] // 128)):
            piece = v[m * 128:(m + 1) * 128]
            if piece.shape[0] < 128:
                piece = jnp.concatenate([piece, jnp.zeros((128 - piece.shape[0], 256), BF16)], axis=0)
            out = out + dot(jnp.where(line == m, 1.0, 0.0).astype(BF16), piece, NT)
        pad = -(-R // 128) * 128
        if pad > R:
            extra = jnp.concatenate([extra, jnp.zeros((1, pad - R), F32)], axis=1)
        for m in range(pad // 128):
            out = out + jnp.where(line8 == m, extra[:, m * 128:(m + 1) * 128], 0.0)
        return out

    def rows_from(tile, count):
        flat = jnp.concatenate([tile[m:m + 1] for m in range(8)], axis=1)
        return [(flat if q == 0 else pltpu.roll(flat, 1024 - q * R, 1))[:, :R] for q in range(count)]

    def columns_of(values):
        n = len(values)
        place = lax.broadcasted_iota(jnp.int32, (8, R), 0)
        v = jnp.zeros((8, R), F32)
        for q, val in enumerate(values):
            v = jnp.where(place == q, val, v)
        v = halves(v, 0)
        line = lax.broadcasted_iota(jnp.int32, (16, 128 * n), 0) % 8
        lanes = lax.broadcasted_iota(jnp.int32, (16, 128 * n), 1)
        pick = jnp.where((lanes >= line * 128) & (lanes < line * 128 + 128), 1.0, 0.0).astype(BF16)
        c = dot(v, pick, TN)
        return [c[:, 128 * q:128 * q + 128] for q in range(n)]

    def wide(c):
        return jnp.concatenate([c] * (total // 128), axis=1)

    def start(k):
        load_copy(k).wait()
        send_edges(0, k, load_v[pl.ds(k * R, R), :])

    def solve_coarse(t, k, c):
        cown[t, k] = c
        cg[t, k, row] = jnp.concatenate([c * m for m in masks], axis=0)
        spread(cg, cg_ss, cg_rs, t, k, "gy")

    def local_part(t, k, r, rsb):
        u = wrow * dot(rsb, inv_v[...], NN)
        send_edges(1 + 2 * t, k, u)
        ur[t, k] = u
        gp[t, k] = fold(r * u)

    def first_local(k):
        wait_edges(0, k)
        r = with_edges(0, k, load_v[pl.ds(k * R, R), :])
        rsb = (wrow * r).astype(BF16)
        c = dot(phi2, rsb, NT)
        solve_coarse(0, k, c[:prim] + c[prim:])
        rr[k] = r
        if k == 0:
            inv_copy.wait()
        local_part(0, k, r, rsb)

    def middle(t, k):
        gathered(cg, cg_ss, cg_rs, t, k, "gy")
        e = cg[t, k, 0]
        cs = [e[:prim] + e[prim:]]
        for j in range(1, ngy):
            o = cg[t, k, j]
            cs.append(o[:prim] + o[prim:])
            e = e + o
        eg[t, k, col] = e.astype(BF16)
        spread(eg, eg_ss, eg_rs, t, k, "gx")
        x2s[...] = dot(l2_r[0], jnp.concatenate(cs, axis=0), NN, HIGH)
        x2 = x2s[pl.ds(pl.multiple_of(row * prim, prim), prim), :]
        xs[t, k] = x2
        for e_ in range(2):
            @pl.when(exists[e_])
            def _():
                x_copy(t, k, e_, e_ ^ 1).start()
        before = x2s[pl.ds(pl.multiple_of(jnp.maximum(row - 1, 0) * prim, prim), prim), :]
        after = x2s[pl.ds(pl.multiple_of(jnp.minimum(row + 1, ngy - 1) * prim, prim), prim), :]
        xown[t, k, 0] = x2
        xown[t, k, 1] = before
        xown[t, k, 2] = after

    def bases_here():
        for e_ in range(4):
            @pl.when(exists[e_])
            def _():
                base_copy(e_, e_).wait_recv()
            at = prow * (1 + e_)
            base = bases[e_]
            pbig[at:at + prow, base:base + 256] = put_back(pr[e_], e_)
        pbigb[...] = pbig[...].astype(BF16)
        pplain[...] = jnp.concatenate([pbig[prow * i:prow * i + prim, :] for i in range(5)], axis=0).astype(BF16)

    def direction(t, k):
        gathered(eg, eg_ss, eg_rs, t, k, "gx")
        e = jnp.concatenate([eg[t, k, i] for i in range(ngx)], axis=0)
        t3s[...] = dot(l3_r[...], e, NN)

        def t3(i):
            return t3s[pl.ds(pl.multiple_of(i * block, block), block), :]

        here, behind, ahead = t3(col), t3(jnp.maximum(col - 1, 0)), t3(jnp.minimum(col + 1, ngx - 1))
        for e_ in range(2):
            @pl.when(exists[e_])
            def _():
                x_copy(t, k, e_, e_).wait_recv()
        own = xown[t, k, 0]
        x = jnp.concatenate(
            [own, here, xr[t, k, 0], behind, xr[t, k, 1], ahead, xown[t, k, 1], here, xown[t, k, 2], here], axis=0
        )
        full = own
        for q, m in enumerate(masks):
            full = full + m * here[q * prim:(q + 1) * prim]
        c = cown[t, k]
        if t == 0:
            xall[k] = x
            xfull[k] = full
        else:
            alpha = tot[k, 2:3]
            x = xall[k] - alpha * x
            full = xfull[k] - alpha * full
            c = cown[0, k] - alpha * c
        coarse = dot(x.astype(BF16), pbigb[...], TN)
        extra = jnp.sum(c * full, axis=0, keepdims=True)
        wait_edges(1 + 2 * t, k)
        z = with_edges(1 + 2 * t, k, ur[t, k] + coarse)
        return z, extra

    def message(t, k, parts, extra):
        sa[t, k, row] = tile_of(parts, extra)
        spread(sa, sa_ss, sa_rs, t, k, "gy")

    def coarse_copy(k, e, there):
        return pltpu.make_async_remote_copy(
            src_ref=ns.at[k, e], dst_ref=nr.at[k, there], send_sem=ns_sem.at[k, e], recv_sem=nr_sem.at[k, there],
            device_id=near(e), device_id_type=MESH,
        )

    def first_apply(k):
        if k == 0:
            bases_here()
        z, extra = direction(0, k)
        if k == 0:
            stiff_copy.wait()
        y = dot(z.astype(BF16), stiff_v[...], NN)
        y0r[k] = y
        z0r[k] = z
        message(0, k, [gp[0, k], fold(z * y)], extra)
        ct = dot(pplain[...], y.astype(BF16), NT)
        cown[1, k] = ct[:prim]
        for e in (2, 3, 0, 1):
            ns[k, e] = ct[prim * (1 + e):prim * (2 + e)]

            @pl.when(exists[e])
            def _():
                coarse_copy(k, e, e ^ 1).start()
        send_edges(2, k, y)

    def coarse_start(k):
        c = cown[1, k]
        for e in range(4):
            @pl.when(exists[e])
            def _():
                coarse_copy(k, e, e).wait_recv()
            c = c + nr[k, e]
        solve_coarse(1, k, c)

    def second_apply(k):
        z, extra = direction(1, k)
        y = dot(z.astype(BF16), stiff_v[...], NN)
        message(1, k, [gp[1, k], fold(z * y), fold(z * y0r[k] + z0r[k] * y)], extra)
        z1r[k] = z

    def relay(t, k):
        gathered(sa, sa_ss, sa_rs, t, k, "gy")
        s = sa[t, k, 0]
        for j in range(1, ngy):
            s = s + sa[t, k, j]
        sb[t, k, col] = s
        spread(sb, sb_ss, sb_rs, t, k, "gx")

    def summed(t, k):
        gathered(sb, sb_ss, sb_rs, t, k, "gx")
        s = sb[t, k, 0]
        for j in range(1, ngx):
            s = s + sb[t, k, j]
        return rows_from(s, 2 + t)

    def second_local(k):
        gamma, delta = summed(0, k)
        rate = gamma / delta
        tot[k, 0:1] = gamma
        tot[k, 1:2] = delta
        tot[k, 2:3] = rate
        alpha, = columns_of([rate])
        wait_edges(2, k)
        r = rr[k] - wide(alpha) * with_edges(2, k, y0r[k])
        local_part(1, k, r, (wrow * r).astype(BF16))

    def out_copy(k):
        return pltpu.make_async_copy(out_v.at[pl.ds(k * R, R)], out_h.at[0, 0, pl.ds(k * R, R)], out_sem.at[k])

    def finish(k):
        gamma, delta, rate = tot[k, 0:1], tot[k, 1:2], tot[k, 2:3]
        new, along, across = summed(1, k)
        beta = new / gamma
        alpha1 = new / (along + beta * across + beta * beta * delta)
        first, second = columns_of([rate + alpha1 * beta, alpha1])
        out_v[pl.ds(k * R, R), :] = wide(first) * z0r[k] + wide(second) * z1r[k]
        out_copy(k).start()

    steps = [
        start, first_local, functools.partial(middle, 0), first_apply, functools.partial(relay, 0), coarse_start,
        second_local, functools.partial(middle, 1), second_apply, functools.partial(relay, 1), finish,
    ]
    for index, step in enumerate(steps):
        for k in range(CHUNKS):
            step(k)

    for k in range(CHUNKS):
        out_copy(k).wait()
        for e in range(4):
            @pl.when(exists[e])
            def _():
                for x in range(4):
                    edge_copy(x, k, e).wait_send()
                coarse_copy(k, e, e ^ 1).wait_send()
                if k == 0:
                    base_copy(e, e ^ 1).wait_send()
                if e < 2:
                    for t in range(2):
                        x_copy(t, k, e, e ^ 1).wait_send()
        for t in range(2):
            sent(cg, cg_ss, cg_rs, t, k, "gy")
            sent(eg, eg_ss, eg_rs, t, k, "gx")
            sent(sa, sa_ss, sa_rs, t, k, "gy")
            sent(sb, sb_ss, sb_rs, t, k, "gx")


def body(load, stiffness, local_inverse, phi, level2_inverse, level3_inverse, aggregate):
    rows, total = load.shape[2:]
    prim = phi.shape[2]
    ngx, ngy = lax.axis_size("gx"), lax.axis_size("gy")
    R, C, block = rows // CHUNKS, CHUNKS, NAGG * prim
    prow = prim + block
    dma = pltpu.SemaphoreType.DMA
    vmem = pltpu.VMEM
    anyw = pl.BlockSpec(memory_space=pl.ANY)
    here = pl.BlockSpec(memory_space=pltpu.VMEM)
    scratch = [
        vmem((rows, total), F32), vmem((total, total), BF16), vmem((total, total), BF16), vmem((rows, total), F32),
        dma((2 + C,)), dma((C,)),
        vmem((4, C, 4, R + R // 2, 128), BF16), vmem((4, C, 4, R + R // 2, 128), BF16), dma((4, C, 4)), dma((4, C, 4)),
        vmem((4, prow, 256), F32), vmem((4, prow, 256), F32), dma((4,)), dma((4,)), vmem((5 * prow, total), F32),
        vmem((5 * prow, total), BF16), vmem((5 * prim, total), BF16),
        vmem((C, 4, prim, R), F32), vmem((C, 4, prim, R), F32), dma((C, 4)), dma((C, 4)),
        vmem((2, C, ngy, block, R), F32), dma((2, C, ngy)), dma((2, C, ngy)),
        vmem((2, C, ngx, block, R), BF16), dma((2, C, ngx)), dma((2, C, ngx)),
        vmem((2, C, prim, R), F32), vmem((2, C, 2, prim, R), F32), dma((2, C, 2)), dma((2, C, 2)),
        vmem((ngy * prim, R), F32), vmem((ngx * block, R), F32),
        vmem((2, C, ngy, 8, 128), F32), dma((2, C, ngy)), dma((2, C, ngy)),
        vmem((2, C, ngx, 8, 128), F32), dma((2, C, ngx)), dma((2, C, ngx)),
        vmem((C, R, total), F32), vmem((2, C, R, total), F32), vmem((C, R, total), F32), vmem((C, R, total), F32),
        vmem((C, R, total), F32), vmem((2, C, R, 128), F32), vmem((2, C, prim, R), F32), vmem((2, C, 3, prim, R), F32),
        vmem((C, 5 * prow, R), F32), vmem((C, prim, R), F32), vmem((C, 8, R), F32),
    ]
    return pl.pallas_call(
        functools.partial(kernel, ngx, ngy, rows, total, prim),
        out_shape=jax.ShapeDtypeStruct((1, 1, rows, total), F32),
        in_specs=[anyw, anyw, anyw, here, here, here, pl.BlockSpec(memory_space=pltpu.SMEM)],
        out_specs=anyw,
        scratch_shapes=scratch,
        compiler_params=pltpu.CompilerParams(
            collective_id=0, has_side_effects=True, vmem_limit_bytes=60 * 1024 * 1024
        ),
    )(load, stiffness, local_inverse, phi, level2_inverse, level3_inverse, aggregate)


def solution(mesh):
    return jax.shard_map(
        body,
        mesh=mesh,
        in_specs=(
            P("gx", "gy", None, None),
            P("gx", "gy", None, None),
            P("gx", "gy", None, None),
            P("gx", "gy", None, None),
            P("gx", None, None),
            P(),
            P("gx", "gy"),
        ),
        out_specs=P("gx", "gy", None, None),
        check_vma=False,
    )
```

```python
import functools

import jax
import jax.numpy as jnp
from jax import lax
from jax.experimental import pallas as pl
from jax.experimental.pallas import tpu as pltpu
from jax.sharding import PartitionSpec as P

NAGG = 2
CHUNKS = 2
HIGH = lax.Precision.HIGHEST
MESH = pl.DeviceIdType.MESH
F32 = jnp.float32
BF16 = jnp.bfloat16
NEAR = (("gx", -1), ("gx", 1), ("gy", -1), ("gy", 1))


def dot(left, right, dims, precision=None):
    return lax.dot_general(
        left, right, (dims, ((), ())), precision=precision, preferred_element_type=F32
    )


NT = ((1,), (1,))
NN = ((1,), (0,))
TN = ((0,), (0,))


def kernel(
    ngx, ngy, rows, total, prim,
    load_h, stiff_h, inv_h, phi_r, l2_r, l3_r, agg_r,
    out_h,
    load_v, stiff_v, inv_v, in_sem,
    es, er, es_sem, er_sem,
    ps, pr, ps_sem, pr_sem, pbig, pbigb, pplain,
    ns, nr, ns_sem, nr_sem,
    cg, cg_ss, cg_rs, eg, eg_ss, eg_rs, xs, xr, xs_sem, xr_sem,
    x2s, t3s,
    sa, sa_ss, sa_rs, sb, sb_ss, sb_rs,
    rr, ur, z0r, z1r, y0r, gp, cown, xown, xall, xfull, tot,
):
    width = total // 4
    R = rows // CHUNKS
    block = NAGG * prim
    col = lax.axis_index("gx")
    row = lax.axis_index("gy")
    exists = (col > 0, col < ngx - 1, row > 0, row < ngy - 1)

    def near(e):
        axis, step = NEAR[e]
        return {axis: (col if axis == "gx" else row) + step}

    def load_copy(k):
        return pltpu.make_async_copy(
            load_h.at[0, 0, pl.ds(k * R, R)], load_v.at[pl.ds(k * R, R)], in_sem.at[2 + k]
        )

    for k in range(CHUNKS):
        load_copy(k).start()
    inv_copy = pltpu.make_async_copy(inv_h.at[0, 0], inv_v, in_sem.at[0])
    stiff_copy = pltpu.make_async_copy(stiff_h.at[0, 0], stiff_v, in_sem.at[1])
    inv_copy.start()
    stiff_copy.start()

    for e in range(4):
        @pl.when(jnp.logical_not(exists[e]))
        def _():
            er[:, :, e] = jnp.zeros((4, CHUNKS) + er.shape[3:], BF16)
            pr[e] = jnp.zeros(pr.shape[1:], F32)
            nr[:, e] = jnp.zeros((CHUNKS,) + nr.shape[2:], F32)
            if e < 2:
                xr[:, :, e] = jnp.zeros((2, CHUNKS) + xr.shape[3:], F32)

    barrier = pltpu.get_barrier_semaphore()
    for d in range(1, ngx):
        pl.semaphore_signal(barrier, inc=1, device_id={"gx": lax.rem(col + d, ngx)}, device_id_type=MESH)
    for d in range(1, ngy):
        pl.semaphore_signal(barrier, inc=1, device_id={"gy": lax.rem(row + d, ngy)}, device_id_type=MESH)

    lane = lax.broadcasted_iota(jnp.int32, (1, total), 1)
    ew = [jnp.where(x, 0.5, 1.0).astype(F32) for x in exists]
    wrow = jnp.where(
        lane < 2 * width,
        jnp.where(lane < width, ew[0], ew[1]),
        jnp.where(lane < 3 * width, ew[2], ew[3]),
    )
    hw = total // 2
    bases = (0, 128, hw, hw + 128)
    wx, wy = wrow[:, :hw], wrow[:, hw:]
    lane128 = lax.broadcasted_iota(jnp.int32, (1, 128), 1)
    low = lane128 < 64
    low192 = lax.broadcasted_iota(jnp.int32, (1, 256), 1) < 192

    def aligned(x, e):
        part = x[:, 128 * (e % 2):128 * (e % 2) + 256]
        return pltpu.roll(part, 192, 1) if e % 2 else part

    def put_back(part, e):
        part = jnp.where(low192, part, 0.0)
        return pltpu.roll(part, 64, 1) if e % 2 else part

    def pack(x, e):
        a = aligned(x, e)
        first, second = a[:, :128], a[:, 128:]
        return first, jnp.where(low, second[: R // 2], pltpu.roll(second[R // 2:], 64, 1))

    def edge_copy(x, k, e):
        return pltpu.make_async_remote_copy(
            src_ref=es.at[x, k, e], dst_ref=er.at[x, k, e ^ 1],
            send_sem=es_sem.at[x, k, e], recv_sem=er_sem.at[x, k, e ^ 1],
            device_id=near(e), device_id_type=MESH,
        )

    def edge_wait(x, k, e):
        return pltpu.make_async_remote_copy(
            src_ref=es.at[x, k, e], dst_ref=er.at[x, k, e],
            send_sem=es_sem.at[x, k, e], recv_sem=er_sem.at[x, k, e],
            device_id=near(e), device_id_type=MESH,
        )

    def send_edges(x, k, part, s):
        for e in (2 * s, 2 * s + 1):
            a, b = pack(part, e)
            es[x, k, e, :R] = a.astype(BF16)
            es[x, k, e, R:] = b.astype(BF16)

            @pl.when(exists[e])
            def _():
                edge_copy(x, k, e).start()

    def with_edges(x, k, part, s):
        added = []
        for e in (2 * s, 2 * s + 1):
            @pl.when(exists[e])
            def _():
                edge_wait(x, k, e).wait_recv()
        for e in (2 * s, 2 * s + 1):
            a = er[x, k, e, :R].astype(F32)
            b = er[x, k, e, R:].astype(F32)
            b = jnp.concatenate([b, pltpu.roll(b, 64, 1)], axis=0)
            added.append(put_back(jnp.concatenate([a, b], axis=1), e))
        first, second = added
        return part + jnp.concatenate([first[:, :128], first[:, 128:] + second[:, :128], second[:, 128:]], axis=1)

    phi = phi_r[0, 0]
    phi_hi = phi.astype(BF16)
    phi_lo = (phi - phi_hi.astype(F32)).astype(BF16)
    phi2 = jnp.concatenate([phi_hi, phi_lo], axis=0)
    masks = [jnp.where(agg_r[0, 0] == q, 1.0, 0.0).astype(F32) for q in range(NAGG)]
    pown = jnp.concatenate([phi] + [phi * m for m in masks], axis=0) * wrow
    prow = pown.shape[0]
    pbig[...] = jnp.zeros_like(pbig)
    pbig[0:prow, :] = pown
    for e in range(4):
        ps[e] = aligned(pown[:, hw * (e // 2):hw * (e // 2) + hw], e)

    def base_copy(e, there):
        return pltpu.make_async_remote_copy(
            src_ref=ps.at[e], dst_ref=pr.at[there], send_sem=ps_sem.at[e], recv_sem=pr_sem.at[there],
            device_id=near(e), device_id_type=MESH,
        )

    pl.semaphore_wait(barrier, ngx - 1 + ngy - 1)
    for e in range(4):
        @pl.when(exists[e])
        def _():
            base_copy(e, e ^ 1).start()

    def spread(buf, ssem, rsem, t, k, axis):
        me, n = (col, ngx) if axis == "gx" else (row, ngy)
        for d in range(1, n):
            pltpu.make_async_remote_copy(
                src_ref=buf.at[t, k, me], dst_ref=buf.at[t, k, me],
                send_sem=ssem.at[t, k, d], recv_sem=rsem.at[t, k, me],
                device_id={axis: lax.rem(me + d, n)}, device_id_type=MESH,
            ).start()

    def gathered(buf, ssem, rsem, t, k, axis):
        me, n = (col, ngx) if axis == "gx" else (row, ngy)
        for d in range(1, n):
            src = lax.rem(me + d, n)
            pltpu.make_async_remote_copy(
                src_ref=buf.at[t, k, src], dst_ref=buf.at[t, k, src],
                send_sem=ssem.at[t, k, d], recv_sem=rsem.at[t, k, src],
                device_id={axis: src}, device_id_type=MESH,
            ).wait_recv()

    def sent(buf, ssem, rsem, t, k, axis):
        me, n = (col, ngx) if axis == "gx" else (row, ngy)
        for d in range(1, n):
            pltpu.make_async_remote_copy(
                src_ref=buf.at[t, k, me], dst_ref=buf.at[t, k, me],
                send_sem=ssem.at[t, k, d], recv_sem=rsem.at[t, k, me],
                device_id={axis: lax.rem(me + d, n)}, device_id_type=MESH,
            ).wait_send()

    def x_copy(t, k, e, there):
        return pltpu.make_async_remote_copy(
            src_ref=xs.at[t, k], dst_ref=xr.at[t, k, there],
            send_sem=xs_sem.at[t, k, e], recv_sem=xr_sem.at[t, k, there],
            device_id=near(e), device_id_type=MESH,
        )

    def fold(v):
        acc = v[:, :128]
        for i in range(128, v.shape[1], 128):
            acc = acc + v[:, i:i + 128]
        return acc

    def halves(v, axis):
        hi = v.astype(BF16)
        return jnp.concatenate([hi, (v - hi.astype(F32)).astype(BF16)], axis=axis)

    line8 = lax.broadcasted_iota(jnp.int32, (8, 128), 0)

    def tile_of(parts, extra):
        v = halves(jnp.concatenate(parts, axis=0), 1)
        line = lax.broadcasted_iota(jnp.int32, (8, 256), 0)
        out = jnp.zeros((8, 128), F32)
        for m in range(-(-v.shape[0] // 128)):
            piece = v[m * 128:(m + 1) * 128]
            if piece.shape[0] < 128:
                piece = jnp.concatenate([piece, jnp.zeros((128 - piece.shape[0], 256), BF16)], axis=0)
            out = out + dot(jnp.where(line == m, 1.0, 0.0).astype(BF16), piece, NT)
        pad = -(-R // 128) * 128
        if pad > R:
            extra = jnp.concatenate([extra, jnp.zeros((1, pad - R), F32)], axis=1)
        for m in range(pad // 128):
            out = out + jnp.where(line8 == m, extra[:, m * 128:(m + 1) * 128], 0.0)
        return out

    def rows_from(tile, count):
        flat = jnp.concatenate([tile[m:m + 1] for m in range(8)], axis=1)
        return [(flat if q == 0 else pltpu.roll(flat, 1024 - q * R, 1))[:, :R] for q in range(count)]

    def columns_of(values):
        n = len(values)
        place = lax.broadcasted_iota(jnp.int32, (8, R), 0)
        v = jnp.zeros((8, R), F32)
        for q, val in enumerate(values):
            v = jnp.where(place == q, val, v)
        v = halves(v, 0)
        line = lax.broadcasted_iota(jnp.int32, (16, 128 * n), 0) % 8
        lanes = lax.broadcasted_iota(jnp.int32, (16, 128 * n), 1)
        pick = jnp.where((lanes >= line * 128) & (lanes < line * 128 + 128), 1.0, 0.0).astype(BF16)
        c = dot(v, pick, TN)
        return [c[:, 128 * q:128 * q + 128] for q in range(n)]

    def wide(c):
        return jnp.concatenate([c] * (hw // 128), axis=1)

    def start(k):
        load_copy(k).wait()
        v = load_v[pl.ds(k * R, R), :]
        send_edges(0, k, v[:, hw:], 1)
        send_edges(0, k, v[:, :hw], 0)

    def solve_coarse(t, k, c):
        cown[t, k] = c
        cg[t, k, row] = jnp.concatenate([c * m for m in masks], axis=0)
        spread(cg, cg_ss, cg_rs, t, k, "gy")

    def local_rest(t, k, rx, ry, sy, acc):
        uy = wy * (acc[:, hw:] + dot(sy, inv_v[hw:, hw:], NN))
        send_edges(1 + 2 * t, k, uy, 1)
        ux = wx * (acc[:, :hw] + dot(sy, inv_v[hw:, :hw], NN))
        send_edges(1 + 2 * t, k, ux, 0)
        ur[t, k, :, hw:] = uy
        ur[t, k, :, :hw] = ux
        gp[t, k] = fold(rx * ux) + fold(ry * uy)

    def first_local(k):
        v = load_v[pl.ds(k * R, R), :]
        rx = with_edges(0, k, v[:, :hw], 0)
        sx = (wx * rx).astype(BF16)
        rr[k, :, :hw] = rx
        if k == 0:
            inv_copy.wait()
        c = dot(phi2[:, :hw], sx, NT)
        acc = dot(sx, inv_v[:hw, :], NN)
        ry = with_edges(0, k, v[:, hw:], 1)
        sy = (wy * ry).astype(BF16)
        rr[k, :, hw:] = ry
        c = c + dot(phi2[:, hw:], sy, NT)
        solve_coarse(0, k, c[:prim] + c[prim:])
        local_rest(0, k, rx, ry, sy, acc)

    def middle(t, k):
        gathered(cg, cg_ss, cg_rs, t, k, "gy")
        e = cg[t, k, 0]
        cs = [e[:prim] + e[prim:]]
        for j in range(1, ngy):
            o = cg[t, k, j]
            cs.append(o[:prim] + o[prim:])
            e = e + o
        eg[t, k, col] = e.astype(BF16)
        spread(eg, eg_ss, eg_rs, t, k, "gx")
        x2s[...] = dot(l2_r[0], jnp.concatenate(cs, axis=0), NN, HIGH)
        x2 = x2s[pl.ds(pl.multiple_of(row * prim, prim), prim), :]
        xs[t, k] = x2
        for e_ in range(2):
            @pl.when(exists[e_])
            def _():
                x_copy(t, k, e_, e_ ^ 1).start()
        before = x2s[pl.ds(pl.multiple_of(jnp.maximum(row - 1, 0) * prim, prim), prim), :]
        after = x2s[pl.ds(pl.multiple_of(jnp.minimum(row + 1, ngy - 1) * prim, prim), prim), :]
        xown[t, k, 0] = x2
        xown[t, k, 1] = before
        xown[t, k, 2] = after

    def bases_here():
        for e_ in range(4):
            @pl.when(exists[e_])
            def _():
                base_copy(e_, e_).wait_recv()
            at = prow * (1 + e_)
            base = bases[e_]
            pbig[at:at + prow, base:base + 256] = put_back(pr[e_], e_)
        pbigb[...] = pbig[...].astype(BF16)
        pplain[...] = jnp.concatenate([pbig[prow * i:prow * i + prim, :] for i in range(5)], axis=0).astype(BF16)

    def direction(t, k):
        gathered(eg, eg_ss, eg_rs, t, k, "gx")
        e = jnp.concatenate([eg[t, k, i] for i in range(ngx)], axis=0)
        t3s[...] = dot(l3_r[...], e, NN)

        def t3(i):
            return t3s[pl.ds(pl.multiple_of(i * block, block), block), :]

        here, behind, ahead = t3(col), t3(jnp.maximum(col - 1, 0)), t3(jnp.minimum(col + 1, ngx - 1))
        for e_ in range(2):
            @pl.when(exists[e_])
            def _():
                x_copy(t, k, e_, e_).wait_recv()
        own = xown[t, k, 0]
        x = jnp.concatenate(
            [own, here, xr[t, k, 0], behind, xr[t, k, 1], ahead, xown[t, k, 1], here, xown[t, k, 2], here], axis=0
        )
        full = own
        for q, m in enumerate(masks):
            full = full + m * here[q * prim:(q + 1) * prim]
        c = cown[t, k]
        if t == 0:
            xall[k] = x
            xfull[k] = full
        else:
            alpha = tot[k, 2:3]
            x = xall[k] - alpha * x
            full = xfull[k] - alpha * full
            c = cown[0, k] - alpha * c
        coarse = dot(x.astype(BF16), pbigb[...], TN)
        extra = jnp.sum(c * full, axis=0, keepdims=True)
        z = [
            with_edges(1 + 2 * t, k, ur[t, k, :, s * hw:s * hw + hw] + coarse[:, s * hw:s * hw + hw], s) for s in range(2)
        ]
        return jnp.concatenate(z, axis=1), extra

    def message(t, k, parts, extra):
        sa[t, k, row] = tile_of(parts, extra)
        spread(sa, sa_ss, sa_rs, t, k, "gy")

    def coarse_copy(k, e, there):
        return pltpu.make_async_remote_copy(
            src_ref=ns.at[k, e], dst_ref=nr.at[k, there], send_sem=ns_sem.at[k, e], recv_sem=nr_sem.at[k, there],
            device_id=near(e), device_id_type=MESH,
        )

    def first_apply(k):
        if k == 0:
            bases_here()
        z, extra = direction(0, k)
        if k == 0:
            stiff_copy.wait()
        y = dot(z.astype(BF16), stiff_v[...], NN)
        y0r[k] = y
        z0r[k] = z
        message(0, k, [gp[0, k], fold(z * y)], extra)
        ct = dot(pplain[...], y.astype(BF16), NT)
        cown[1, k] = ct[:prim]
        for e in (2, 3, 0, 1):
            ns[k, e] = ct[prim * (1 + e):prim * (2 + e)]

            @pl.when(exists[e])
            def _():
                coarse_copy(k, e, e ^ 1).start()
        send_edges(2, k, y[:, hw:], 1)
        send_edges(2, k, y[:, :hw], 0)

    def coarse_start(k):
        c = cown[1, k]
        for e in range(4):
            @pl.when(exists[e])
            def _():
                coarse_copy(k, e, e).wait_recv()
            c = c + nr[k, e]
        solve_coarse(1, k, c)

    def second_apply(k):
        z, extra = direction(1, k)
        y = dot(z.astype(BF16), stiff_v[...], NN)
        message(1, k, [gp[1, k], fold(z * y), fold(z * y0r[k] + z0r[k] * y)], extra)
        z1r[k] = z

    def relay(t, k):
        gathered(sa, sa_ss, sa_rs, t, k, "gy")
        s = sa[t, k, 0]
        for j in range(1, ngy):
            s = s + sa[t, k, j]
        sb[t, k, col] = s
        spread(sb, sb_ss, sb_rs, t, k, "gx")

    def summed(t, k):
        gathered(sb, sb_ss, sb_rs, t, k, "gx")
        s = sb[t, k, 0]
        for j in range(1, ngx):
            s = s + sb[t, k, j]
        return rows_from(s, 2 + t)

    def second_local(k):
        gamma, delta = summed(0, k)
        rate = gamma / delta
        tot[k, 0:1] = gamma
        tot[k, 1:2] = delta
        tot[k, 2:3] = rate
        alpha, = columns_of([rate])
        rx = rr[k, :, :hw] - wide(alpha) * with_edges(2, k, y0r[k, :, :hw], 0)
        acc = dot((wx * rx).astype(BF16), inv_v[:hw, :], NN)
        ry = rr[k, :, hw:] - wide(alpha) * with_edges(2, k, y0r[k, :, hw:], 1)
        local_rest(1, k, rx, ry, (wy * ry).astype(BF16), acc)

    def finish(k):
        gamma, delta, rate = tot[k, 0:1], tot[k, 1:2], tot[k, 2:3]
        new, along, across = summed(1, k)
        beta = new / gamma
        alpha1 = new / (along + beta * across + beta * beta * delta)
        first, second = columns_of([rate + alpha1 * beta, alpha1])
        for s in range(2):
            here = slice(s * hw, s * hw + hw)
            out_h[0, 0, pl.ds(k * R, R), here] = wide(first) * z0r[k, :, here] + wide(second) * z1r[k, :, here]

    steps = [
        start, first_local, functools.partial(middle, 0), first_apply, functools.partial(relay, 0), coarse_start,
        second_local, functools.partial(middle, 1), second_apply, functools.partial(relay, 1), finish,
    ]
    for index, step in enumerate(steps):
        for k in range(CHUNKS):
            step(k)

    for k in range(CHUNKS):
        for e in range(4):
            @pl.when(exists[e])
            def _():
                for x in range(4):
                    edge_copy(x, k, e).wait_send()
                coarse_copy(k, e, e ^ 1).wait_send()
                if k == 0:
                    base_copy(e, e ^ 1).wait_send()
                if e < 2:
                    for t in range(2):
                        x_copy(t, k, e, e ^ 1).wait_send()
        for t in range(2):
            sent(cg, cg_ss, cg_rs, t, k, "gy")
            sent(eg, eg_ss, eg_rs, t, k, "gx")
            sent(sa, sa_ss, sa_rs, t, k, "gy")
            sent(sb, sb_ss, sb_rs, t, k, "gx")


def body(load, stiffness, local_inverse, phi, level2_inverse, level3_inverse, aggregate):
    rows, total = load.shape[2:]
    prim = phi.shape[2]
    ngx, ngy = lax.axis_size("gx"), lax.axis_size("gy")
    R, C, block = rows // CHUNKS, CHUNKS, NAGG * prim
    prow = prim + block
    dma = pltpu.SemaphoreType.DMA
    vmem = pltpu.VMEM
    anyw = pl.BlockSpec(memory_space=pl.ANY)
    here = pl.BlockSpec(memory_space=pltpu.VMEM)
    scratch = [
        vmem((rows, total), F32), vmem((total, total), BF16), vmem((total, total), BF16),
        dma((2 + C,)),
        vmem((4, C, 4, R + R // 2, 128), BF16), vmem((4, C, 4, R + R // 2, 128), BF16), dma((4, C, 4)), dma((4, C, 4)),
        vmem((4, prow, 256), F32), vmem((4, prow, 256), F32), dma((4,)), dma((4,)), vmem((5 * prow, total), F32),
        vmem((5 * prow, total), BF16), vmem((5 * prim, total), BF16),
        vmem((C, 4, prim, R), F32), vmem((C, 4, prim, R), F32), dma((C, 4)), dma((C, 4)),
        vmem((2, C, ngy, block, R), F32), dma((2, C, ngy)), dma((2, C, ngy)),
        vmem((2, C, ngx, block, R), BF16), dma((2, C, ngx)), dma((2, C, ngx)),
        vmem((2, C, prim, R), F32), vmem((2, C, 2, prim, R), F32), dma((2, C, 2)), dma((2, C, 2)),
        vmem((ngy * prim, R), F32), vmem((ngx * block, R), F32),
        vmem((2, C, ngy, 8, 128), F32), dma((2, C, ngy)), dma((2, C, ngy)),
        vmem((2, C, ngx, 8, 128), F32), dma((2, C, ngx)), dma((2, C, ngx)),
        vmem((C, R, total), F32), vmem((2, C, R, total), F32), vmem((C, R, total), F32), vmem((C, R, total), F32),
        vmem((C, R, total), F32), vmem((2, C, R, 128), F32), vmem((2, C, prim, R), F32), vmem((2, C, 3, prim, R), F32),
        vmem((C, 5 * prow, R), F32), vmem((C, prim, R), F32), vmem((C, 8, R), F32),
    ]
    return pl.pallas_call(
        functools.partial(kernel, ngx, ngy, rows, total, prim),
        out_shape=pltpu.VMEM((1, 1, rows, total), F32),
        in_specs=[anyw, anyw, anyw, here, here, here, pl.BlockSpec(memory_space=pltpu.SMEM)],
        out_specs=here,
        scratch_shapes=scratch,
        compiler_params=pltpu.CompilerParams(
            collective_id=0, has_side_effects=True, vmem_limit_bytes=60 * 1024 * 1024
        ),
    )(load, stiffness, local_inverse, phi, level2_inverse, level3_inverse, aggregate)


def solution(mesh):
    return jax.shard_map(
        body,
        mesh=mesh,
        in_specs=(
            P("gx", "gy", None, None),
            P("gx", "gy", None, None),
            P("gx", "gy", None, None),
            P("gx", "gy", None, None),
            P("gx", None, None),
            P(),
            P("gx", "gy"),
        ),
        out_specs=P("gx", "gy", None, None),
        check_vma=False,
    )
```

```python
import functools

import jax
import jax.numpy as jnp
from jax import lax
from jax.experimental import pallas as pl
from jax.experimental.pallas import tpu as pltpu
from jax.sharding import PartitionSpec as P

NAGG = 2
CHUNKS = 2
HIGH = lax.Precision.HIGHEST
MESH = pl.DeviceIdType.MESH
F32 = jnp.float32
BF16 = jnp.bfloat16
NEAR = (("gx", -1), ("gx", 1), ("gy", -1), ("gy", 1))


def dot(left, right, dims, precision=None):
    return lax.dot_general(
        left, right, (dims, ((), ())), precision=precision, preferred_element_type=F32
    )


NT = ((1,), (1,))
NN = ((1,), (0,))
TN = ((0,), (0,))


def kernel(
    ngx, ngy, rows, total, prim,
    load_h, stiff_h, inv_h, phi_r, l2_r, l3_r, agg_r,
    out_h,
    load_v, stiff_v, inv_v, in_sem,
    es, er, es_sem, er_sem,
    ps, pr, ps_sem, pr_sem, pbig, pbigb, pplain,
    ns, nr, ns_sem, nr_sem,
    cg, cg_ss, cg_rs, eg, eg_ss, eg_rs, xs, xr, xs_sem, xr_sem,
    x2s, t3s,
    sa, sa_ss, sa_rs, sb, sb_ss, sb_rs,
    rr, ur, z0r, z1r, y0r, gp, cown, xown, acol, xfull, tot,
):
    width = total // 4
    R = rows // CHUNKS
    block = NAGG * prim
    col = lax.axis_index("gx")
    row = lax.axis_index("gy")
    exists = (col > 0, col < ngx - 1, row > 0, row < ngy - 1)

    def near(e):
        axis, step = NEAR[e]
        return {axis: (col if axis == "gx" else row) + step}

    def load_copy(k):
        return pltpu.make_async_copy(
            load_h.at[0, 0, pl.ds(k * R, R)], load_v.at[pl.ds(k * R, R)], in_sem.at[2 + k]
        )

    for k in range(CHUNKS):
        load_copy(k).start()
    inv_copy = pltpu.make_async_copy(inv_h.at[0, 0], inv_v, in_sem.at[0])
    stiff_copy = pltpu.make_async_copy(stiff_h.at[0, 0], stiff_v, in_sem.at[1])
    inv_copy.start()
    stiff_copy.start()

    for e in range(4):
        @pl.when(jnp.logical_not(exists[e]))
        def _():
            er[:, :, e] = jnp.zeros((4, CHUNKS) + er.shape[3:], BF16)
            pr[e] = jnp.zeros(pr.shape[1:], F32)
            nr[:, e] = jnp.zeros((CHUNKS,) + nr.shape[2:], F32)
            if e < 2:
                xr[:, :, e] = jnp.zeros((2, CHUNKS) + xr.shape[3:], F32)

    barrier = pltpu.get_barrier_semaphore()
    for d in range(1, ngx):
        pl.semaphore_signal(barrier, inc=1, device_id={"gx": lax.rem(col + d, ngx)}, device_id_type=MESH)
    for d in range(1, ngy):
        pl.semaphore_signal(barrier, inc=1, device_id={"gy": lax.rem(row + d, ngy)}, device_id_type=MESH)

    lane = lax.broadcasted_iota(jnp.int32, (1, total), 1)
    ew = [jnp.where(x, 0.5, 1.0).astype(F32) for x in exists]
    wrow = jnp.where(
        lane < 2 * width,
        jnp.where(lane < width, ew[0], ew[1]),
        jnp.where(lane < 3 * width, ew[2], ew[3]),
    )
    hw = total // 2
    bases = (0, 128, hw, hw + 128)
    wx, wy = wrow[:, :hw], wrow[:, hw:]
    lane128 = lax.broadcasted_iota(jnp.int32, (1, 128), 1)
    low = lane128 < 64
    low192 = lax.broadcasted_iota(jnp.int32, (1, 256), 1) < 192

    def aligned(x, e):
        part = x[:, 128 * (e % 2):128 * (e % 2) + 256]
        return pltpu.roll(part, 192, 1) if e % 2 else part

    def put_back(part, e):
        part = jnp.where(low192, part, 0.0)
        return pltpu.roll(part, 64, 1) if e % 2 else part

    def pack(x, e):
        a = aligned(x, e)
        first, second = a[:, :128], a[:, 128:]
        return first, jnp.where(low, second[: R // 2], pltpu.roll(second[R // 2:], 64, 1))

    def edge_copy(x, k, e):
        return pltpu.make_async_remote_copy(
            src_ref=es.at[x, k, e], dst_ref=er.at[x, k, e ^ 1],
            send_sem=es_sem.at[x, k, e], recv_sem=er_sem.at[x, k, e ^ 1],
            device_id=near(e), device_id_type=MESH,
        )

    def edge_wait(x, k, e):
        return pltpu.make_async_remote_copy(
            src_ref=es.at[x, k, e], dst_ref=er.at[x, k, e],
            send_sem=es_sem.at[x, k, e], recv_sem=er_sem.at[x, k, e],
            device_id=near(e), device_id_type=MESH,
        )

    def send_edges(x, k, part, s):
        for e in (2 * s, 2 * s + 1):
            a, b = pack(part, e)
            es[x, k, e, :R] = a.astype(BF16)
            es[x, k, e, R:] = b.astype(BF16)

            @pl.when(exists[e])
            def _():
                edge_copy(x, k, e).start()

    def with_edges(x, k, part, s):
        added = []
        for e in (2 * s, 2 * s + 1):
            @pl.when(exists[e])
            def _():
                edge_wait(x, k, e).wait_recv()
        for e in (2 * s, 2 * s + 1):
            a = er[x, k, e, :R].astype(F32)
            b = er[x, k, e, R:].astype(F32)
            b = jnp.concatenate([b, pltpu.roll(b, 64, 1)], axis=0)
            added.append(put_back(jnp.concatenate([a, b], axis=1), e))
        first, second = added
        return part + jnp.concatenate([first[:, :128], first[:, 128:] + second[:, :128], second[:, 128:]], axis=1)

    phi = phi_r[0, 0]
    phi_hi = phi.astype(BF16)
    phi_lo = (phi - phi_hi.astype(F32)).astype(BF16)
    phi2 = jnp.concatenate([phi_hi, phi_lo], axis=0)
    masks = [jnp.where(agg_r[0, 0] == q, 1.0, 0.0).astype(F32) for q in range(NAGG)]
    pown = jnp.concatenate([phi] + [phi * m for m in masks], axis=0) * wrow
    prow = pown.shape[0]
    pbig[...] = jnp.zeros_like(pbig)
    pbig[0:prow, :] = pown
    for e in range(4):
        ps[e] = aligned(pown[:, hw * (e // 2):hw * (e // 2) + hw], e)

    def base_copy(e, there):
        return pltpu.make_async_remote_copy(
            src_ref=ps.at[e], dst_ref=pr.at[there], send_sem=ps_sem.at[e], recv_sem=pr_sem.at[there],
            device_id=near(e), device_id_type=MESH,
        )

    pl.semaphore_wait(barrier, ngx - 1 + ngy - 1)
    for e in range(4):
        @pl.when(exists[e])
        def _():
            base_copy(e, e ^ 1).start()

    def spread(buf, ssem, rsem, t, k, axis):
        me, n = (col, ngx) if axis == "gx" else (row, ngy)
        for d in range(1, n):
            pltpu.make_async_remote_copy(
                src_ref=buf.at[t, k, me], dst_ref=buf.at[t, k, me],
                send_sem=ssem.at[t, k, d], recv_sem=rsem.at[t, k, me],
                device_id={axis: lax.rem(me + d, n)}, device_id_type=MESH,
            ).start()

    def gathered(buf, ssem, rsem, t, k, axis):
        me, n = (col, ngx) if axis == "gx" else (row, ngy)
        for d in range(1, n):
            src = lax.rem(me + d, n)
            pltpu.make_async_remote_copy(
                src_ref=buf.at[t, k, src], dst_ref=buf.at[t, k, src],
                send_sem=ssem.at[t, k, d], recv_sem=rsem.at[t, k, src],
                device_id={axis: src}, device_id_type=MESH,
            ).wait_recv()

    def sent(buf, ssem, rsem, t, k, axis):
        me, n = (col, ngx) if axis == "gx" else (row, ngy)
        for d in range(1, n):
            pltpu.make_async_remote_copy(
                src_ref=buf.at[t, k, me], dst_ref=buf.at[t, k, me],
                send_sem=ssem.at[t, k, d], recv_sem=rsem.at[t, k, me],
                device_id={axis: lax.rem(me + d, n)}, device_id_type=MESH,
            ).wait_send()

    def x_copy(t, k, e, there):
        return pltpu.make_async_remote_copy(
            src_ref=xs.at[t, k], dst_ref=xr.at[t, k, there],
            send_sem=xs_sem.at[t, k, e], recv_sem=xr_sem.at[t, k, there],
            device_id=near(e), device_id_type=MESH,
        )

    def fold(v):
        acc = v[:, :128]
        for i in range(128, v.shape[1], 128):
            acc = acc + v[:, i:i + 128]
        return acc

    def halves(v, axis):
        hi = v.astype(BF16)
        return jnp.concatenate([hi, (v - hi.astype(F32)).astype(BF16)], axis=axis)

    line8 = lax.broadcasted_iota(jnp.int32, (8, 128), 0)

    def tile_of(parts, extra):
        v = halves(jnp.concatenate(parts, axis=0), 1)
        line = lax.broadcasted_iota(jnp.int32, (8, 256), 0)
        out = jnp.zeros((8, 128), F32)
        for m in range(-(-v.shape[0] // 128)):
            piece = v[m * 128:(m + 1) * 128]
            if piece.shape[0] < 128:
                piece = jnp.concatenate([piece, jnp.zeros((128 - piece.shape[0], 256), BF16)], axis=0)
            out = out + dot(jnp.where(line == m, 1.0, 0.0).astype(BF16), piece, NT)
        pad = -(-R // 128) * 128
        if pad > R:
            extra = jnp.concatenate([extra, jnp.zeros((1, pad - R), F32)], axis=1)
        for m in range(pad // 128):
            out = out + jnp.where(line8 == m, extra[:, m * 128:(m + 1) * 128], 0.0)
        return out

    def rows_from(tile, count):
        flat = jnp.concatenate([tile[m:m + 1] for m in range(8)], axis=1)
        return [(flat if q == 0 else pltpu.roll(flat, 1024 - q * R, 1))[:, :R] for q in range(count)]

    def columns_of(values):
        n = len(values)
        place = lax.broadcasted_iota(jnp.int32, (8, R), 0)
        v = jnp.zeros((8, R), F32)
        for q, val in enumerate(values):
            v = jnp.where(place == q, val, v)
        v = halves(v, 0)
        line = lax.broadcasted_iota(jnp.int32, (16, 128 * n), 0) % 8
        lanes = lax.broadcasted_iota(jnp.int32, (16, 128 * n), 1)
        pick = jnp.where((lanes >= line * 128) & (lanes < line * 128 + 128), 1.0, 0.0).astype(BF16)
        c = dot(v, pick, TN)
        return [c[:, 128 * q:128 * q + 128] for q in range(n)]

    def wide(c):
        return jnp.concatenate([c] * (hw // 128), axis=1)

    def start(k):
        load_copy(k).wait()
        v = load_v[pl.ds(k * R, R), :]
        send_edges(0, k, v[:, hw:], 1)
        send_edges(0, k, v[:, :hw], 0)

    def solve_coarse(t, k, c):
        cown[t, k] = c
        cg[t, k, row] = jnp.concatenate([c * m for m in masks], axis=0)
        spread(cg, cg_ss, cg_rs, t, k, "gy")

    def local_rest(t, k, rx, ry, sy, acc):
        uy = wy * (acc[:, hw:] + dot(sy, inv_v[hw:, hw:], NN))
        send_edges(1 + 2 * t, k, uy, 1)
        ux = wx * (acc[:, :hw] + dot(sy, inv_v[hw:, :hw], NN))
        send_edges(1 + 2 * t, k, ux, 0)
        ur[t, k, :, hw:] = uy
        ur[t, k, :, :hw] = ux
        if t == 0:
            gp[t, k] = fold(rx * ux) + fold(ry * uy)

    def first_local(k):
        v = load_v[pl.ds(k * R, R), :]
        rx = with_edges(0, k, v[:, :hw], 0)
        sx = (wx * rx).astype(BF16)
        rr[k, :, :hw] = rx
        if k == 0:
            inv_copy.wait()
        c = dot(phi2[:, :hw], sx, NT)
        acc = dot(sx, inv_v[:hw, :], NN)
        ry = with_edges(0, k, v[:, hw:], 1)
        sy = (wy * ry).astype(BF16)
        rr[k, :, hw:] = ry
        c = c + dot(phi2[:, hw:], sy, NT)
        solve_coarse(0, k, c[:prim] + c[prim:])
        local_rest(0, k, rx, ry, sy, acc)

    def middle(t, k):
        gathered(cg, cg_ss, cg_rs, t, k, "gy")
        e = cg[t, k, 0]
        cs = [e[:prim] + e[prim:]]
        for j in range(1, ngy):
            o = cg[t, k, j]
            cs.append(o[:prim] + o[prim:])
            e = e + o
        eg[t, k, col] = e.astype(BF16)
        spread(eg, eg_ss, eg_rs, t, k, "gx")
        x2s[...] = dot(l2_r[0], jnp.concatenate(cs, axis=0), NN, HIGH)
        x2 = x2s[pl.ds(pl.multiple_of(row * prim, prim), prim), :]
        xs[t, k] = x2
        for e_ in range(2):
            @pl.when(exists[e_])
            def _():
                x_copy(t, k, e_, e_ ^ 1).start()
        before = x2s[pl.ds(pl.multiple_of(jnp.maximum(row - 1, 0) * prim, prim), prim), :]
        after = x2s[pl.ds(pl.multiple_of(jnp.minimum(row + 1, ngy - 1) * prim, prim), prim), :]
        xown[t, k, 0] = x2
        xown[t, k, 1] = before
        xown[t, k, 2] = after

    def bases_here():
        for e_ in range(4):
            @pl.when(exists[e_])
            def _():
                base_copy(e_, e_).wait_recv()
            at = prow * (1 + e_)
            base = bases[e_]
            pbig[at:at + prow, base:base + 256] = put_back(pr[e_], e_)
        pbigb[...] = pbig[...].astype(BF16)
        pplain[...] = jnp.concatenate([pbig[prow * i:prow * i + prim, :] for i in range(5)], axis=0).astype(BF16)

    def direction(t, k):
        gathered(eg, eg_ss, eg_rs, t, k, "gx")
        e = jnp.concatenate([eg[t, k, i] for i in range(ngx)], axis=0)
        t3s[...] = dot(l3_r[...], e, NN)

        def t3(i):
            return t3s[pl.ds(pl.multiple_of(i * block, block), block), :]

        here, behind, ahead = t3(col), t3(jnp.maximum(col - 1, 0)), t3(jnp.minimum(col + 1, ngx - 1))
        for e_ in range(2):
            @pl.when(exists[e_])
            def _():
                x_copy(t, k, e_, e_).wait_recv()
        own = xown[t, k, 0]
        x = jnp.concatenate(
            [own, here, xr[t, k, 0], behind, xr[t, k, 1], ahead, xown[t, k, 1], here, xown[t, k, 2], here], axis=0
        )
        full = own
        for q, m in enumerate(masks):
            full = full + m * here[q * prim:(q + 1) * prim]
        c = cown[t, k]
        if t == 0:
            xfull[k] = full
        else:
            alpha = tot[k, 2:3]
            full = xfull[k] - alpha * full
            c = cown[0, k] - alpha * c
        coarse = dot(x.astype(BF16), pbigb[...], TN)
        extra = jnp.sum(c * full, axis=0, keepdims=True)
        z = [
            with_edges(1 + 2 * t, k, ur[t, k, :, s * hw:s * hw + hw] + coarse[:, s * hw:s * hw + hw], s) for s in range(2)
        ]
        return jnp.concatenate(z, axis=1), extra

    def message(t, k, parts, extra):
        sa[t, k, row] = tile_of(parts, extra)
        spread(sa, sa_ss, sa_rs, t, k, "gy")

    def coarse_copy(k, e, there):
        return pltpu.make_async_remote_copy(
            src_ref=ns.at[k, e], dst_ref=nr.at[k, there], send_sem=ns_sem.at[k, e], recv_sem=nr_sem.at[k, there],
            device_id=near(e), device_id_type=MESH,
        )

    def first_apply(k):
        if k == 0:
            bases_here()
        z, extra = direction(0, k)
        if k == 0:
            stiff_copy.wait()
        y = dot(z.astype(BF16), stiff_v[...], NN)
        y0r[k] = y
        z0r[k] = z
        message(0, k, [gp[0, k], fold(z * y)], extra)
        ct = dot(pplain[...], y.astype(BF16), NT)
        cown[1, k] = ct[:prim]
        for e in (2, 3, 0, 1):
            ns[k, e] = ct[prim * (1 + e):prim * (2 + e)]

            @pl.when(exists[e])
            def _():
                coarse_copy(k, e, e ^ 1).start()
        send_edges(2, k, y[:, hw:], 1)
        send_edges(2, k, y[:, :hw], 0)

    def coarse_start(k):
        c = cown[1, k]
        for e in range(4):
            @pl.when(exists[e])
            def _():
                coarse_copy(k, e, e).wait_recv()
            c = c + nr[k, e]
        solve_coarse(1, k, c)

    def second_apply(k):
        z, extra = direction(1, k)
        a = wide(acol[k])
        z = z0r[k] - jnp.concatenate([a, a], axis=1) * z
        y = dot(z.astype(BF16), stiff_v[...], NN)
        message(1, k, [gp[1, k], fold(z * y), fold(z * y0r[k] + z0r[k] * y)], extra)
        z1r[k] = z

    def relay(t, k):
        gathered(sa, sa_ss, sa_rs, t, k, "gy")
        s = sa[t, k, 0]
        for j in range(1, ngy):
            s = s + sa[t, k, j]
        sb[t, k, col] = s
        spread(sb, sb_ss, sb_rs, t, k, "gx")

    def summed(t, k):
        gathered(sb, sb_ss, sb_rs, t, k, "gx")
        s = sb[t, k, 0]
        for j in range(1, ngx):
            s = s + sb[t, k, j]
        return rows_from(s, 2 + t)

    def second_local(k):
        rows_k = pl.ds(k * R, R)
        sx = with_edges(2, k, y0r[k, :, :hw], 0)
        load_v[rows_k, :hw] = sx
        acc = dot((wx * sx).astype(BF16), inv_v[:hw, :], NN)
        sy = with_edges(2, k, y0r[k, :, hw:], 1)
        load_v[rows_k, hw:] = sy
        local_rest(1, k, sx, sy, (wy * sy).astype(BF16), acc)

    def first_rate(k):
        gamma, delta = summed(0, k)
        rate = gamma / delta
        tot[k, 0:1] = gamma
        tot[k, 1:2] = delta
        tot[k, 2:3] = rate
        alpha, = columns_of([rate])
        acol[k] = alpha
        part = jnp.zeros((R, 128), F32)
        for s in range(2):
            at = slice(s * hw, s * hw + hw)
            a = wide(alpha)
            part = part + fold((rr[k, :, at] - a * load_v[pl.ds(k * R, R), at]) * (ur[0, k, :, at] - a * ur[1, k, :, at]))
        gp[1, k] = part

    def finish(k):
        gamma, delta, rate = tot[k, 0:1], tot[k, 1:2], tot[k, 2:3]
        new, along, across = summed(1, k)
        beta = new / gamma
        alpha1 = new / (along + beta * across + beta * beta * delta)
        first, second = columns_of([rate + alpha1 * beta, alpha1])
        for s in range(2):
            here = slice(s * hw, s * hw + hw)
            out_h[0, 0, pl.ds(k * R, R), here] = wide(first) * z0r[k, :, here] + wide(second) * z1r[k, :, here]

    steps = [
        start, first_local, functools.partial(middle, 0), first_apply, functools.partial(relay, 0), coarse_start,
        second_local, functools.partial(middle, 1), first_rate, second_apply, functools.partial(relay, 1), finish,
    ]
    for index, step in enumerate(steps):
        for k in range(CHUNKS):
            step(k)

    for k in range(CHUNKS):
        for e in range(4):
            @pl.when(exists[e])
            def _():
                for x in range(4):
                    edge_copy(x, k, e).wait_send()
                coarse_copy(k, e, e ^ 1).wait_send()
                if k == 0:
                    base_copy(e, e ^ 1).wait_send()
                if e < 2:
                    for t in range(2):
                        x_copy(t, k, e, e ^ 1).wait_send()
        for t in range(2):
            sent(cg, cg_ss, cg_rs, t, k, "gy")
            sent(eg, eg_ss, eg_rs, t, k, "gx")
            sent(sa, sa_ss, sa_rs, t, k, "gy")
            sent(sb, sb_ss, sb_rs, t, k, "gx")


def body(load, stiffness, local_inverse, phi, level2_inverse, level3_inverse, aggregate):
    rows, total = load.shape[2:]
    prim = phi.shape[2]
    ngx, ngy = lax.axis_size("gx"), lax.axis_size("gy")
    R, C, block = rows // CHUNKS, CHUNKS, NAGG * prim
    prow = prim + block
    dma = pltpu.SemaphoreType.DMA
    vmem = pltpu.VMEM
    anyw = pl.BlockSpec(memory_space=pl.ANY)
    here = pl.BlockSpec(memory_space=pltpu.VMEM)
    scratch = [
        vmem((rows, total), F32), vmem((total, total), BF16), vmem((total, total), BF16),
        dma((2 + C,)),
        vmem((4, C, 4, R + R // 2, 128), BF16), vmem((4, C, 4, R + R // 2, 128), BF16), dma((4, C, 4)), dma((4, C, 4)),
        vmem((4, prow, 256), F32), vmem((4, prow, 256), F32), dma((4,)), dma((4,)), vmem((5 * prow, total), F32),
        vmem((5 * prow, total), BF16), vmem((5 * prim, total), BF16),
        vmem((C, 4, prim, R), F32), vmem((C, 4, prim, R), F32), dma((C, 4)), dma((C, 4)),
        vmem((2, C, ngy, block, R), F32), dma((2, C, ngy)), dma((2, C, ngy)),
        vmem((2, C, ngx, block, R), BF16), dma((2, C, ngx)), dma((2, C, ngx)),
        vmem((2, C, prim, R), F32), vmem((2, C, 2, prim, R), F32), dma((2, C, 2)), dma((2, C, 2)),
        vmem((ngy * prim, R), F32), vmem((ngx * block, R), F32),
        vmem((2, C, ngy, 8, 128), F32), dma((2, C, ngy)), dma((2, C, ngy)),
        vmem((2, C, ngx, 8, 128), F32), dma((2, C, ngx)), dma((2, C, ngx)),
        vmem((C, R, total), F32), vmem((2, C, R, total), F32), vmem((C, R, total), F32), vmem((C, R, total), F32),
        vmem((C, R, total), F32), vmem((2, C, R, 128), F32), vmem((2, C, prim, R), F32), vmem((2, C, 3, prim, R), F32),
        vmem((C, R, 128), F32), vmem((C, prim, R), F32), vmem((C, 8, R), F32),
    ]
    return pl.pallas_call(
        functools.partial(kernel, ngx, ngy, rows, total, prim),
        out_shape=pltpu.VMEM((1, 1, rows, total), F32),
        in_specs=[anyw, anyw, anyw, here, here, here, pl.BlockSpec(memory_space=pltpu.SMEM)],
        out_specs=here,
        scratch_shapes=scratch,
        compiler_params=pltpu.CompilerParams(
            collective_id=0, has_side_effects=True, vmem_limit_bytes=60 * 1024 * 1024
        ),
    )(load, stiffness, local_inverse, phi, level2_inverse, level3_inverse, aggregate)


def solution(mesh):
    return jax.shard_map(
        body,
        mesh=mesh,
        in_specs=(
            P("gx", "gy", None, None),
            P("gx", "gy", None, None),
            P("gx", "gy", None, None),
            P("gx", "gy", None, None),
            P("gx", None, None),
            P(),
            P("gx", "gy"),
        ),
        out_specs=P("gx", "gy", None, None),
        check_vma=False,
    )
```
